256 devices in a mesh: rows: 16 (over y_lo, z), cols: 16 (over x, y_hi, core).
Axes of the slice: x: 4, y: 4 (y_hi: 2, y_lo: 2; y = y_hi * 2 + y_lo), z: 8, core: 2. Of those that a mesh axis runs over, the one named last changes fastest.
Arguments:
- matrix: bfloat16 [4096, 32768], P('rows', 'cols'), may hold values from -0.125 to 0.125
- inverse: bfloat16 [32768, 32768], P('rows', 'cols'), may hold values from -1 to 1
- target: float32 [4096, 128], P('rows'), may hold values from -60 to 60
- penalty: float32 [128], replicated, may hold values from 0.5 to 16
- consensus: float32 [32768, 128], P('cols'), may hold values from -6 to 6
- copy_duals: float32 [16, 32768, 128], P('rows', 'cols'), may hold values from -6 to 6
- fit_parts: float32 [16, 4096, 128], P('cols', 'rows'), may hold values from -6 to 6
- fit_mean: float32 [4096, 128], P('rows'), may hold values from -3 to 3
- fit_duals: float32 [4096, 128], P('rows'), may hold values from -3 to 3
Outputs:
- coefficients: float32 [32768, 128], P('cols')
- fitted: float32 [4096, 128], P('rows')
- history: float32 [5, 2], replicated
The draws below stay inside these ranges and needn't reach their ends.
All inputs are finite; a program needn't handle non-finite values.
Results may differ from the reference program's by a relative error of at most 0.006.
Values sent between devices are 32-bit elements; how exact they have to be, the bound alone decides.
A program may use at most 64 MiB of HBM per device.

```python
import math
import jax
import jax.numpy as jnp
from jax import lax

COLS_DEV = 2048
ROWS_DEV = 256
TARGETS = 128
ITERS = 5
ALL_ROWS = 4096
ALL_COLS = 32768
N_ROWS = 16
N_COLS = 16


def draw_inverse(key, part):
    noise_key, scale_key = jax.random.split(jax.random.fold_in(key, 11))
    shape = (N_ROWS, COLS_DEV, N_COLS, COLS_DEV)
    entries = jax.random.normal(noise_key, shape, jnp.float32)
    levels = jax.random.uniform(scale_key, (N_ROWS, COLS_DEV, N_COLS, 1), jnp.float32, 0.5, 1.0)
    entries = jnp.clip(entries, -6.0, 6.0) * (0.2 / math.sqrt(COLS_DEV))
    identity = jnp.eye(COLS_DEV, dtype=jnp.float32)[None, :, None, :]
    result = entries * (1.0 - identity) + identity * levels
    return result.reshape(N_ROWS * COLS_DEV, N_COLS * COLS_DEV).astype(jnp.bfloat16)


def draw_target(key, part):
    noise_key = jax.random.fold_in(jax.random.fold_in(key, 23), 0)
    rising = jnp.power(3.0, jnp.arange(ALL_ROWS, dtype=jnp.float32) / ALL_ROWS)
    values = jax.random.truncated_normal(noise_key, -6.0, 6.0, (ALL_ROWS, TARGETS), jnp.float32)
    return values * rising[:, None]


def block_levels(stream_key, shape, pieces, smallest, high):
    level, own = 1.0, jax.random.fold_in(stream_key, 6)
    for dim, blocks in pieces:
        steps = jnp.exp(jax.random.uniform(jax.random.fold_in(own, dim), (blocks,), jnp.float32, smallest / len(pieces), high / len(pieces)))
        level = level * jnp.repeat(steps, shape[dim] // blocks).reshape([-1 if axis == dim else 1 for axis in range(len(shape))])
    return level


def noise(rng, extent, scale, bound, pieces=(), kind=jnp.bfloat16):
    values = scale * jax.random.normal(rng, extent, jnp.float32)
    if pieces:
        values = values * block_levels(rng, extent, pieces, -0.22, 0.18)
    return jnp.clip(values, -bound, bound).astype(kind)


def setup_inputs(seed: int = 0) -> dict:
    key_list = jax.random.split(jax.random.key(seed), 10)
    return {
        "matrix": noise(key_list[0], (ALL_ROWS, ALL_COLS), COLS_DEV ** -0.5, 0.125, ((0, 16), (1, 16))),
        "inverse": draw_inverse(jax.random.fold_in(key_list[9], 71), 0),
        "target": draw_target(jax.random.fold_in(key_list[9], 71), 0),
        "penalty": jnp.clip(jnp.exp(jax.random.uniform(key_list[3], (TARGETS,), jnp.float32, math.log(0.5), math.log(16.0))), 0.5, 16.0),
        "consensus": noise(key_list[4], (ALL_COLS, TARGETS), 1.0, 6.0, ((0, 16),), jnp.float32),
        "copy_duals": noise(key_list[5], (N_ROWS, ALL_COLS, TARGETS), 0.5, 6.0, ((0, 16), (1, 16)), jnp.float32),
        "fit_parts": noise(key_list[6], (N_COLS, ALL_ROWS, TARGETS), 1.0, 6.0, ((0, 16), (1, 16)), jnp.float32),
        "fit_mean": noise(key_list[7], (ALL_ROWS, TARGETS), 0.2, 3.0, ((0, 16),), jnp.float32),
        "fit_duals": noise(key_list[8], (ALL_ROWS, TARGETS), 0.2, 3.0, ((0, 16),), jnp.float32),
    }


def reference(matrix, inverse, target, penalty, consensus, copy_duals, fit_parts, fit_mean, fit_duals):
    blocks = matrix.reshape(N_ROWS, ROWS_DEV, N_COLS, COLS_DEV)
    caches = inverse.reshape(N_ROWS, COLS_DEV, N_COLS, COLS_DEV)
    center = consensus.reshape(N_COLS, COLS_DEV, TARGETS)
    duals = copy_duals.reshape(N_ROWS, N_COLS, COLS_DEV, TARGETS)
    shares = jnp.transpose(fit_parts.reshape(N_COLS, N_ROWS, ROWS_DEV, TARGETS), (1, 0, 2, 3))
    observed = target.reshape(N_ROWS, ROWS_DEV, TARGETS)
    fitted_mean = fit_mean.reshape(N_ROWS, ROWS_DEV, TARGETS)
    row_dual = fit_duals.reshape(N_ROWS, ROWS_DEV, TARGETS)
    threshold = penalty / N_ROWS
    normalizer = N_ROWS * ALL_COLS * TARGETS
    mean_share = jnp.sum(shares, axis=1) / N_COLS
    records = []
    for iteration in range(ITERS):
        offsets = (shares - mean_share[:, None] + fitted_mean[:, None] - row_dual[:, None]).astype(jnp.bfloat16)

        def project(operands):
            tile_rows, cached, offset_row, dual_row = operands
            tile_float = tile_rows.astype(jnp.float32)
            pulled = jnp.einsum("rjc,jrt->jct", tile_float, offset_row.astype(jnp.float32))
            right_side = lax.optimization_barrier((center - dual_row + pulled).astype(jnp.bfloat16))
            copies = jnp.einsum("cjd,jdt->jct", cached.astype(jnp.float32), right_side.astype(jnp.float32))
            rounded = lax.optimization_barrier(copies.astype(jnp.bfloat16))
            fresh_shares = jnp.einsum("rjc,jct->jrt", tile_float, rounded.astype(jnp.float32))
            return copies, fresh_shares

        copies, shares = lax.map(project, (blocks, caches, offsets, duals))
        mean_share = jnp.sum(shares, axis=1) / N_COLS
        average = jnp.sum(copies + duals, axis=0) / N_ROWS
        updated = average - jnp.clip(average, -threshold, threshold)
        motion = N_ROWS * jnp.sum((updated - center) ** 2)
        center = updated
        fitted_mean = (observed + row_dual + mean_share) / (N_COLS + 1)
        spread = jnp.sum((copies - center[None]) ** 2) + N_COLS * jnp.sum((mean_share - fitted_mean) ** 2)
        records.append(jnp.stack([spread, motion]) / normalizer)
        duals = duals + copies - center[None]
        row_dual = row_dual + mean_share - fitted_mean
    history = jnp.stack(records)
    return center.reshape(ALL_COLS, TARGETS), (fitted_mean * N_COLS).reshape(ALL_ROWS, TARGETS), history
```

```python
import jax
import jax.numpy as jnp
from jax import lax
from jax.experimental import pallas as pl
from jax.experimental.pallas import tpu as pltpu
from jax.sharding import Mesh
from jax.sharding import PartitionSpec as P

ITERS = 5
ROWS = ("rows_0", "rows_1")
COLS = ("cols_0", "cols_1", "cols_2")
AXES = ("rows_0", "rows_1", "cols_0", "cols_1", "cols_2")
SIZES = (2, 8, 4, 2, 2)
MESH = pl.DeviceIdType.MESH

WIDTH = 2048
HEIGHT = 256
TARGETS = 128
NZ = 8
CHUNKS = 4
CHUNK = WIDTH // CHUNKS
PIECE = CHUNK // NZ
HALF = HEIGHT // 2
QUARTER = HALF // 4
LOADS = 9
NORMALIZER = 16.0 * 32768.0 * 128.0


def kernel(
    inverse_hbm, matrix_hbm, target_hbm, penalty_ref, consensus_hbm, duals_hbm, parts_hbm, mean_hbm, fit_duals_hbm,
    coef_hbm, fitted_ref, history_ref,
    cache, tile, tile_t, center, dual, summed, copies, pulled, right_side, rounded,
    share, share_mean, fitted_mean, row_dual, observed,
    chain, y_out, y_in, core_in, x_in, half_sum, quarter_sum, yh_in, record, record_in,
    load_sem, cache_sem, store_sem,
    rs_send, rs_recv, ag_send, ag_recv, y_send, y_recv, s_send, s_recv, h_send, h_recv,
):
    me = tuple(lax.axis_index(axis) for axis in AXES)
    my_y, my_z, my_x, my_yh, my_core = me

    def device(**moved):
        return tuple(moved.get(axis, index) for axis, index in zip(AXES, me))

    def z_at(offset):
        return lax.rem(my_z + offset + 2 * NZ, NZ)

    core_peer = device(cols_2=1 - my_core)
    yh_peer = device(cols_1=1 - my_yh)
    y_peer = device(rows_0=1 - my_y)

    def x_peer(step):
        return device(cols_0=lax.rem(my_x + step, 4))

    peers = [core_peer, yh_peer, y_peer]
    peers += [x_peer(step) for step in range(1, 4)]
    peers += [device(rows_1=z_at(step)) for step in range(1, NZ)]
    barrier = pltpu.get_barrier_semaphore()
    for peer in peers:
        pl.semaphore_signal(barrier, inc=1, device_id=peer, device_id_type=MESH)

    loads = [
        pltpu.make_async_copy(src, dst, load_sem.at[index])
        for index, (src, dst) in enumerate(
            (
                (parts_hbm.at[0], share),
                (matrix_hbm, tile),
                (mean_hbm, fitted_mean),
                (fit_duals_hbm, row_dual),
                (consensus_hbm, center.at[1]),
                (duals_hbm.at[0], dual),
                (target_hbm, observed),
            )
        )
    ]
    for load in loads:
        load.start()

    def cache_load(chunk):
        rows = pl.ds(chunk * CHUNK, CHUNK)
        return pltpu.make_async_copy(inverse_hbm.at[rows], cache.at[rows], cache_sem.at[chunk])

    for chunk in range(CHUNKS):
        cache_load(chunk).start()

    def remote(src, dst, send, recv, where):
        return pltpu.make_async_remote_copy(
            src_ref=src, dst_ref=dst, send_sem=send, recv_sem=recv, device_id=where, device_id_type=MESH
        )

    mine = pl.ds(my_core * HALF, HALF)
    other = pl.ds((1 - my_core) * HALF, HALF)

    def quarter(x_index):
        return pl.ds(x_index * QUARTER, QUARTER)

    def piece_of_mean(x_index):
        return pl.ds(my_core * HALF + x_index * QUARTER, QUARTER)

    def core_sum(par):
        return remote(share.at[other], core_in.at[par], s_send.at[par, 0], s_recv.at[par, 0], core_peer)

    def x_sum(par, step):
        return remote(
            half_sum.at[quarter(lax.rem(my_x + step, 4))], x_in.at[par, step - 1],
            s_send.at[par, step], s_recv.at[par, step], x_peer(step),
        )

    def yh_sum(par):
        return remote(quarter_sum, yh_in.at[par], s_send.at[par, 4], s_recv.at[par, 4], yh_peer)

    def x_copy(par, step):
        return remote(
            share_mean.at[par, piece_of_mean(my_x)], share_mean.at[par, piece_of_mean(my_x)],
            s_send.at[par, 4 + step], s_recv.at[par, 4 + step], x_peer(step),
        )

    def core_copy(par):
        return remote(
            share_mean.at[par, mine], share_mean.at[par, mine], s_send.at[par, 8], s_recv.at[par, 8], core_peer
        )

    def stage_a(par):
        core_sum(par).start()

    def stage_b(par):
        core_sum(par).wait()
        half_sum[...] = share[mine, :] + core_in[par]
        for step in range(1, 4):
            x_sum(par, step).start()

    def stage_c(par):
        for step in range(1, 4):
            x_sum(par, step).wait()
        quarter_sum[...] = half_sum[quarter(my_x), :] + (x_in[par, 0] + x_in[par, 1] + x_in[par, 2])
        yh_sum(par).start()

    def stage_d(par):
        yh_sum(par).wait()
        share_mean[par, piece_of_mean(my_x), :] = (quarter_sum[...] + yh_in[par]) * (1.0 / 16)
        for step in range(1, 4):
            x_copy(par, step).start()

    def stage_e(par):
        for step in range(1, 4):
            x_copy(par, step).wait()
        core_copy(par).start()

    def stage_f(par):
        core_copy(par).wait()

    def pull(par):
        offsets = (share[...] - share_mean[par] + fitted_mean[...] - row_dual[...]).astype(jnp.bfloat16)
        pulled[...] = jnp.dot(tile_t[...], offsets, preferred_element_type=jnp.float32)

    loads[0].wait()
    pl.semaphore_wait(barrier, len(peers))
    stage_a(1)
    loads[1].wait()
    for block in range(WIDTH // HEIGHT):
        columns = slice(block * HEIGHT, (block + 1) * HEIGHT)
        tile_t[columns, :] = tile[:, columns].T
    stage_b(1)
    for load in loads[2:]:
        load.wait()
    record[...] = jnp.zeros_like(record)
    stage_c(1)
    stage_d(1)
    stage_e(1)
    stage_f(1)
    pull(1)
    for chunk in range(CHUNKS):
        rows = slice(chunk * CHUNK, (chunk + 1) * CHUNK)
        right_side[rows, :] = (center[1, rows, :] - dual[rows, :] + pulled[rows, :]).astype(jnp.bfloat16)
    threshold = penalty_ref[...] * (1.0 / 16)
    for chunk in range(CHUNKS):
        cache_load(chunk).wait()

    def turn(chunk):
        return 1 - 2 * lax.rem(chunk, 2)

    def piece(chunk, z_index):
        return pl.ds(pl.multiple_of(chunk * CHUNK + z_index * PIECE, PIECE), PIECE)

    def along(chunk, sign):
        return device(rows_1=z_at(sign * turn(chunk)))

    def first_hop(par, chunk, sign):
        slot, far = (0, 4) if sign > 0 else (4, -3)
        return remote(
            summed.at[piece(chunk, z_at(far * turn(chunk)))], chain.at[par, chunk, slot],
            rs_send.at[par, chunk, slot], rs_recv.at[par, chunk, slot], along(chunk, sign),
        )

    def next_hop(par, chunk, slot, sign):
        return remote(
            chain.at[par, chunk, slot - 1], chain.at[par, chunk, slot],
            rs_send.at[par, chunk, slot], rs_recv.at[par, chunk, slot], along(chunk, sign),
        )

    def add_here(par, chunk, slot, offset):
        chain[par, chunk, slot] = chain[par, chunk, slot] + summed[piece(chunk, z_at(offset * turn(chunk))), :]

    def y_swap(par, chunk):
        return remote(y_out.at[par, chunk], y_in.at[par, chunk], y_send.at[par, chunk], y_recv.at[par, chunk], y_peer)

    def spread_hop(par, chunk, hop, sign):
        slot = hop if sign > 0 else 4 + hop
        where = piece(chunk, z_at(-sign * hop * turn(chunk)))
        return remote(
            center.at[par, where], center.at[par, where],
            ag_send.at[par, chunk, slot], ag_recv.at[par, chunk, slot], along(chunk, sign),
        )

    def each_chunk(body):
        def step(chunk, carry):
            body(chunk)
            return carry

        lax.fori_loop(0, CHUNKS, step, 0)

    def in_rows(values):
        return jnp.sum(values.reshape(-1, 8, TARGETS), axis=0)

    def iteration(k, carry):
        par = lax.rem(k, 2)
        old = 1 - par

        def multiply(chunk):
            rows = pl.ds(pl.multiple_of(chunk * CHUNK, CHUNK), CHUNK)
            product = jnp.dot(cache[rows, :], right_side[...], preferred_element_type=jnp.float32)
            copies[rows, :] = product
            rounded[rows, :] = product.astype(jnp.bfloat16)
            summed[rows, :] = product + dual[rows, :]
            first_hop(par, chunk, 1).start()
            first_hop(par, chunk, -1).start()

        each_chunk(multiply)
        share[...] = jnp.dot(tile[...], rounded[...], preferred_element_type=jnp.float32)
        stage_a(par)

        def second(chunk):
            first_hop(par, chunk, 1).wait_recv()
            add_here(par, chunk, 0, 3)
            next_hop(par, chunk, 1, 1).start()
            first_hop(par, chunk, -1).wait_recv()
            add_here(par, chunk, 4, -2)
            next_hop(par, chunk, 5, -1).start()

        each_chunk(second)
        stage_b(par)

        def third(chunk):
            next_hop(par, chunk, 1, 1).wait_recv()
            add_here(par, chunk, 1, 2)
            next_hop(par, chunk, 2, 1).start()
            next_hop(par, chunk, 5, -1).wait_recv()
            add_here(par, chunk, 5, -1)
            next_hop(par, chunk, 6, -1).start()

        each_chunk(third)
        stage_c(par)

        def fourth(chunk):
            next_hop(par, chunk, 2, 1).wait_recv()
            add_here(par, chunk, 2, 1)
            next_hop(par, chunk, 3, 1).start()

        each_chunk(fourth)
        stage_d(par)

        def owned(chunk):
            next_hop(par, chunk, 6, -1).wait_recv()
            next_hop(par, chunk, 3, 1).wait_recv()
            y_out[par, chunk] = summed[piece(chunk, my_z), :] + (chain[par, chunk, 3] + chain[par, chunk, 6])
            y_swap(par, chunk).start()

        each_chunk(owned)
        stage_e(par)

        def update(chunk, motion):
            y_swap(par, chunk).wait_recv()
            average = (y_out[par, chunk] + y_in[par, chunk]) * (1.0 / 16)
            updated = average - jnp.clip(average, -threshold, threshold)
            where = piece(chunk, my_z)
            center[par, where, :] = updated
            spread_hop(par, chunk, 0, 1).start()
            spread_hop(par, chunk, 0, -1).start()
            return motion + in_rows((updated - center[old, where, :]) ** 2)

        motion = lax.fori_loop(0, CHUNKS, update, jnp.zeros((8, TARGETS), jnp.float32))
        stage_f(par)

        for hop in range(1, 4):

            def forward(chunk):
                spread_hop(par, chunk, hop - 1, 1).wait_recv()
                spread_hop(par, chunk, hop, 1).start()
                spread_hop(par, chunk, hop - 1, -1).wait_recv()
                if hop < 3:
                    spread_hop(par, chunk, hop, -1).start()

            each_chunk(forward)
            if hop == 1:
                fitted = (observed[...] + row_dual[...] + share_mean[par]) * (1.0 / 17)
                drift = share_mean[par] - fitted
                fitted_mean[...] = fitted
                row_dual[...] = row_dual[...] + drift
                spread_rows = in_rows(drift**2)
                pull(par)

        def finish(chunk, spread):
            spread_hop(par, chunk, 3, 1).wait_recv()
            rows = pl.ds(pl.multiple_of(chunk * CHUNK, CHUNK), CHUNK)
            new = center[par, rows, :]
            new_dual = summed[rows, :] - new
            dual[rows, :] = new_dual
            right_side[rows, :] = (new - new_dual + pulled[rows, :]).astype(jnp.bfloat16)
            return spread + in_rows((copies[rows, :] - new) ** 2)

        spread = lax.fori_loop(0, CHUNKS, finish, spread_rows)

        def sent(chunk):
            first_hop(par, chunk, 1).wait_send()
            first_hop(par, chunk, -1).wait_send()
            for slot, sign in ((1, 1), (2, 1), (3, 1), (5, -1), (6, -1)):
                next_hop(par, chunk, slot, sign).wait_send()
            y_swap(par, chunk).wait_send()
            for hop in range(4):
                spread_hop(par, chunk, hop, 1).wait_send()
            for hop in range(3):
                spread_hop(par, chunk, hop, -1).wait_send()

        each_chunk(sent)
        row = lax.broadcasted_iota(jnp.int32, (8, TARGETS), 0)
        lane = lax.broadcasted_iota(jnp.int32, (8, TARGETS), 1)
        spread_here = jnp.where((row == k) & (lane == 0), jnp.sum(spread), 0.0)
        motion_here = jnp.where((row == k) & (lane == 1), 8.0 * jnp.sum(motion), 0.0)
        record[...] = record[...] + (spread_here + motion_here)
        return carry

    lax.fori_loop(0, ITERS, iteration, 0)

    last = (ITERS - 1) % 2
    store = pltpu.make_async_copy(center.at[last], coef_hbm, store_sem)
    store.start()
    fitted_ref[...] = fitted_mean[...] * 16.0

    slot = 0
    for axis, size in (("rows_1", 8), ("rows_0", 2), ("cols_0", 4), ("cols_1", 2), ("cols_2", 2)):
        index = lax.axis_index(axis)
        swaps = []
        for step in range(1, size):
            there = lax.rem(index + step, size)
            arriving = lax.rem(index + size - step, size)
            swaps.append(
                (
                    remote(
                        record, record_in.at[slot + index], h_send.at[slot + step], h_recv.at[slot + index],
                        device(**{axis: there}),
                    ),
                    remote(
                        record, record_in.at[slot + arriving], h_send.at[slot + step], h_recv.at[slot + arriving],
                        device(**{axis: there}),
                    ),
                )
            )
        for going, coming in swaps:
            going.start()
        record_in[slot + index] = record[...]
        for going, coming in swaps:
            coming.wait_recv()
        for going, coming in swaps:
            going.wait_send()
        total = record_in[slot]
        for part in range(1, size):
            total = total + record_in[slot + part]
        record[...] = total
        slot += size
    history_ref[...] = record[0:ITERS, 0:2] * (1.0 / NORMALIZER)
    store.wait()


def local(matrix, inverse, target, penalty, consensus, copy_duals, fit_parts, fit_mean, fit_duals):
    f32, bf16 = jnp.float32, jnp.bfloat16
    anywhere = pl.BlockSpec(memory_space=pl.ANY)
    inside = pl.BlockSpec(memory_space=pltpu.VMEM)
    dma = pltpu.SemaphoreType.DMA

    def v(*shape, dtype=f32):
        return pltpu.VMEM(shape, dtype)

    return pl.pallas_call(
        kernel,
        name="admm",
        out_shape=(
            jax.ShapeDtypeStruct((WIDTH, TARGETS), f32),
            jax.ShapeDtypeStruct((HEIGHT, TARGETS), f32),
            jax.ShapeDtypeStruct((ITERS, 2), f32),
        ),
        in_specs=[anywhere, anywhere, anywhere, inside, anywhere, anywhere, anywhere, anywhere, anywhere],
        out_specs=(anywhere, inside, inside),
        scratch_shapes=[
            v(WIDTH, WIDTH, dtype=bf16),
            v(HEIGHT, WIDTH, dtype=bf16),
            v(WIDTH, HEIGHT, dtype=bf16),
            v(2, WIDTH, TARGETS),
            v(WIDTH, TARGETS),
            v(WIDTH, TARGETS),
            v(WIDTH, TARGETS),
            v(WIDTH, TARGETS),
            v(WIDTH, TARGETS, dtype=bf16),
            v(WIDTH, TARGETS, dtype=bf16),
            v(HEIGHT, TARGETS),
            v(2, HEIGHT, TARGETS),
            v(HEIGHT, TARGETS),
            v(HEIGHT, TARGETS),
            v(HEIGHT, TARGETS),
            v(2, CHUNKS, 7, PIECE, TARGETS),
            v(2, CHUNKS, PIECE, TARGETS),
            v(2, CHUNKS, PIECE, TARGETS),
            v(2, HALF, TARGETS),
            v(2, 3, QUARTER, TARGETS),
            v(HALF, TARGETS),
            v(QUARTER, TARGETS),
            v(2, QUARTER, TARGETS),
            v(8, TARGETS),
            v(18, 8, TARGETS),
            dma((LOADS,)),
            dma((CHUNKS,)),
            dma,
            dma((2, CHUNKS, 7)),
            dma((2, CHUNKS, 7)),
            dma((2, CHUNKS, 7)),
            dma((2, CHUNKS, 7)),
            dma((2, CHUNKS)),
            dma((2, CHUNKS)),
            dma((2, 9)),
            dma((2, 9)),
            dma((18,)),
            dma((18,)),
        ],
        compiler_params=pltpu.CompilerParams(
            collective_id=0, has_side_effects=True, vmem_limit_bytes=48 * 1024 * 1024
        ),
    )(inverse, matrix, target, penalty.reshape(1, TARGETS), consensus, copy_duals, fit_parts, fit_mean, fit_duals)


def solution(mesh):
    split = Mesh(mesh.devices.reshape(SIZES), AXES)
    return jax.shard_map(
        local,
        mesh=split,
        in_specs=(
            P(ROWS, COLS),
            P(ROWS, COLS),
            P(ROWS, None),
            P(),
            P(COLS, None),
            P(ROWS, COLS, None),
            P(COLS, ROWS, None),
            P(ROWS, None),
            P(ROWS, None),
        ),
        out_specs=(P(COLS, None), P(ROWS, None), P()),
        check_vma=False,
    )
```

```python
import jax
import jax.numpy as jnp
from jax import lax
from jax.experimental import pallas as pl
from jax.experimental.pallas import tpu as pltpu
from jax.sharding import Mesh
from jax.sharding import PartitionSpec as P

ITERS = 5
ROWS = ("rows_0", "rows_1")
COLS = ("cols_0", "cols_1", "cols_2")
AXES = ("rows_0", "rows_1", "cols_0", "cols_1", "cols_2")
SIZES = (2, 8, 4, 2, 2)
MESH = pl.DeviceIdType.MESH
GROUPS = (("cols_2",), ("rows_0",), ("cols_1",), ("cols_0",), ("rows_1",))

WIDTH = 2048
HEIGHT = 256
TARGETS = 128
NZ = 8
CHUNKS = 4
CHUNK = WIDTH // CHUNKS
PIECE = CHUNK // NZ
BLOCK = 512
SMALL = 512
HALF = HEIGHT // 2
QUARTER = HALF // 4
LOADS = 7
FIRST = {0: (1, 3, 1), 3: (-1, -3, 1), 6: (1, 4, 2)}
SPREAD = {0: (1, 0, 1), 1: (1, -1, 1), 2: (1, -2, 1), 3: (-1, 0, 1), 4: (-1, 1, 1), 5: (-1, 2, 1), 6: (1, -2, 2)}
NORMALIZER = 16.0 * 32768.0 * 128.0


def kernel(
    inverse_hbm, matrix_hbm, target_hbm, penalty_ref, consensus_hbm, duals_hbm, parts_hbm, mean_hbm, fit_duals_hbm,
    coef_hbm, fitted_ref, history_ref,
    cache, tile, tile_t, center, dual, summed, copies, pulled, right_side, rounded,
    share, share_mean, fitted_mean, row_dual, observed,
    chain, y_out, y_in, core_in, x_in, half_sum, quarter_sum, yh_in, clip_piece, spread_sum, tally, record, record_in,
    load_sem, cache_sem, store_sem,
    rs_send, rs_recv, ag_send, ag_recv, y_send, y_recv, s_send, s_recv, h_send, h_recv,
):
    me = tuple(lax.axis_index(axis) for axis in AXES)
    my_y, my_z, my_x, my_yh, my_core = me

    def device(**moved):
        return tuple(moved.get(axis, index) for axis, index in zip(AXES, me))

    def z_at(offset):
        return lax.rem(my_z + offset + 2 * NZ, NZ)

    core_peer = device(cols_2=1 - my_core)
    yh_peer = device(cols_1=1 - my_yh)
    y_peer = device(rows_0=1 - my_y)

    def x_peer(step):
        return device(cols_0=lax.rem(my_x + step, 4))

    def group(stage):
        axes = GROUPS[stage]
        size, index = 1, 0
        for axis in axes:
            extent = SIZES[AXES.index(axis)]
            size, index = size * extent, index * extent + me[AXES.index(axis)]
        members = {}
        for step in range(1, size):
            rest, moved = lax.rem(index + step, size), {}
            for axis in reversed(axes):
                extent = SIZES[AXES.index(axis)]
                moved[axis] = lax.rem(rest, extent)
                rest = lax.div(rest, extent)
            members[step] = device(**moved)
        return size, index, members

    peers = [peer for stage in range(len(GROUPS)) for peer in group(stage)[2].values()]
    barrier = pltpu.get_barrier_semaphore()
    for peer in peers:
        pl.semaphore_signal(barrier, inc=1, device_id=peer, device_id_type=MESH)

    loads = [
        pltpu.make_async_copy(src, dst, load_sem.at[index])
        for index, (src, dst) in enumerate(
            (
                (parts_hbm.at[0], share),
                (matrix_hbm, tile),
                (mean_hbm, fitted_mean),
                (fit_duals_hbm, row_dual),
                (consensus_hbm, center.at[1]),
                (duals_hbm.at[0], dual),
                (target_hbm, observed),
            )
        )
    ]
    for load in loads:
        load.start()

    def cache_load(chunk):
        rows = pl.ds(chunk * CHUNK, CHUNK)
        return pltpu.make_async_copy(inverse_hbm.at[rows], cache.at[rows], cache_sem.at[chunk])

    for chunk in range(CHUNKS):
        cache_load(chunk).start()

    def remote(src, dst, send, recv, where):
        return pltpu.make_async_remote_copy(
            src_ref=src, dst_ref=dst, send_sem=send, recv_sem=recv, device_id=where, device_id_type=MESH
        )

    mine = pl.ds(my_core * HALF, HALF)
    other = pl.ds((1 - my_core) * HALF, HALF)

    def quarter(x_index):
        return pl.ds(x_index * QUARTER, QUARTER)

    def piece_of_mean(x_index):
        return pl.ds(my_core * HALF + x_index * QUARTER, QUARTER)

    def core_sum(par):
        return remote(share.at[other], core_in.at[par], s_send.at[par, 0], s_recv.at[par, 0], core_peer)

    def x_sum(par, step):
        return remote(
            half_sum.at[quarter(lax.rem(my_x + step, 4))], x_in.at[par, step - 1],
            s_send.at[par, step], s_recv.at[par, step], x_peer(step),
        )

    def yh_sum(par):
        return remote(quarter_sum, yh_in.at[par], s_send.at[par, 4], s_recv.at[par, 4], yh_peer)

    def x_copy(par, step):
        return remote(
            share_mean.at[par, piece_of_mean(my_x)], share_mean.at[par, piece_of_mean(my_x)],
            s_send.at[par, 4 + step], s_recv.at[par, 4 + step], x_peer(step),
        )

    def core_copy(par):
        return remote(
            share_mean.at[par, mine], share_mean.at[par, mine], s_send.at[par, 8], s_recv.at[par, 8], core_peer
        )

    def stage_a(par):
        core_sum(par).start()

    def stage_b(par):
        core_sum(par).wait()
        half_sum[...] = share[mine, :] + core_in[par]
        for step in range(1, 4):
            x_sum(par, step).start()

    def stage_c(par):
        for step in range(1, 4):
            x_sum(par, step).wait()
        quarter_sum[...] = half_sum[quarter(my_x), :] + (x_in[par, 0] + x_in[par, 1] + x_in[par, 2])
        yh_sum(par).start()

    def stage_d(par):
        yh_sum(par).wait()
        share_mean[par, piece_of_mean(my_x), :] = (quarter_sum[...] + yh_in[par]) * (1.0 / 16)
        for step in range(1, 4):
            x_copy(par, step).start()

    def stage_e(par):
        for step in range(1, 4):
            x_copy(par, step).wait()
        core_copy(par).start()

    def stage_f(par):
        core_copy(par).wait()

    def pull(par):
        offsets = (share[...] - share_mean[par] + fitted_mean[...] - row_dual[...]).astype(jnp.bfloat16)
        pulled[...] = jnp.dot(tile_t[...], offsets, preferred_element_type=jnp.float32)

    loads[0].wait()
    pl.semaphore_wait(barrier, len(peers))
    stage_a(1)
    loads[1].wait()

    def transpose_block(block, carry):
        columns = pl.ds(pl.multiple_of(block * HEIGHT, HEIGHT), HEIGHT)
        tile_t[columns, :] = tile[:, columns].T
        return carry

    lax.fori_loop(0, WIDTH // HEIGHT, transpose_block, 0)
    stage_b(1)
    for load in loads[2:]:
        load.wait()
    record[...] = jnp.zeros_like(record)
    clip_piece[...] = jnp.zeros_like(clip_piece)
    stage_c(1)
    stage_d(1)
    stage_e(1)
    stage_f(1)
    pull(1)

    def first_right_side(block, carry):
        rows = pl.ds(pl.multiple_of(block * HEIGHT, HEIGHT), HEIGHT)
        right_side[rows, :] = (center[1, rows, :] - dual[rows, :] + pulled[rows, :]).astype(jnp.bfloat16)
        return carry

    lax.fori_loop(0, WIDTH // HEIGHT, first_right_side, 0)
    threshold = penalty_ref[...] * (1.0 / 16)
    for chunk in range(CHUNKS):
        cache_load(chunk).wait()

    z_near = {offset: z_at(offset) for offset in range(-4, 5)}
    z_device = {offset: device(rows_1=z_near[offset]) for offset in (-2, -1, 1, 2)}

    def turn(chunk):
        return 1 - 2 * (chunk % 2)

    def piece(chunk, offset):
        return pl.ds(pl.multiple_of(chunk * CHUNK + z_near[offset] * PIECE, PIECE), PIECE)

    def first_hop(par, chunk, slot):
        sign, far, hops = FIRST[slot]
        way = turn(chunk)
        return remote(
            summed.at[piece(chunk, far * way)], chain.at[par, chunk, slot],
            rs_send.at[par, chunk, slot], rs_recv.at[par, chunk, slot], z_device[sign * hops * way],
        )

    def next_hop(par, chunk, slot):
        sign = 1 if slot < 3 else -1
        return remote(
            chain.at[par, chunk, slot - 1], chain.at[par, chunk, slot],
            rs_send.at[par, chunk, slot], rs_recv.at[par, chunk, slot], z_device[sign * turn(chunk)],
        )

    def add_here(par, chunk, slot, offset):
        total = chain[par, chunk, slot] + summed[piece(chunk, offset * turn(chunk)), :]
        chain[par, chunk, slot] = total if slot > 0 else total + chain[par, chunk, 6]

    def y_swap(par, chunk):
        return remote(y_out.at[par, chunk], y_in.at[par, chunk], y_send.at[par, chunk], y_recv.at[par, chunk], y_peer)

    def spread_hop(par, chunk, slot):
        sign, owner, hops = SPREAD[slot]
        way = turn(chunk)
        where = piece(chunk, owner * way)
        return remote(
            center.at[par, where], center.at[par, where],
            ag_send.at[par, chunk, slot], ag_recv.at[par, chunk, slot], z_device[sign * hops * way],
        )

    def in_rows(values):
        return jnp.sum(values.reshape(-1, 8, TARGETS), axis=0)

    def chunk_rows(chunk):
        return slice(chunk * CHUNK, (chunk + 1) * CHUNK)

    def note(row, lane, value):
        rows = lax.broadcasted_iota(jnp.int32, (8, TARGETS), 0)
        lanes = lax.broadcasted_iota(jnp.int32, (8, TARGETS), 1)
        record[...] = record[...] + jnp.where((rows == row) & (lanes == lane), jnp.sum(value), 0.0)

    first_slot = (0, 2, 4, 6, 10)

    def record_swaps(stage):
        slot = first_slot[stage]
        size, index, members = group(stage)
        swaps = []
        for step in range(1, size):
            arriving = lax.rem(index + size - step, size)
            swaps.append(
                tuple(
                    remote(
                        record, record_in.at[slot + at], h_send.at[slot + step], h_recv.at[slot + at], members[step]
                    )
                    for at in (index, arriving)
                )
            )
        return slot, size, index, swaps

    def record_start(stage):
        slot, size, index, swaps = record_swaps(stage)
        for going, coming in swaps:
            going.start()
        record_in[slot + index] = record[...]

    def record_finish(stage):
        slot, size, index, swaps = record_swaps(stage)
        for going, coming in swaps:
            coming.wait_recv()
        for going, coming in swaps:
            going.wait_send()
        total = record_in[slot]
        for part in range(1, size):
            total = total + record_in[slot + part]
        record[...] = total

    def first_hops(par, chunk):
        way = 1 - 2 * lax.rem(chunk, 2)
        for slot in (6, 0, 3):
            sign, far, hops = FIRST[slot]
            where = pl.ds(pl.multiple_of(chunk * CHUNK + z_at(far * way) * PIECE, PIECE), PIECE)
            remote(
                summed.at[where], chain.at[par, chunk, slot],
                rs_send.at[par, chunk, slot], rs_recv.at[par, chunk, slot], device(rows_1=z_at(sign * hops * way)),
            ).start()

    def sums_sent(par):
        for chunk in range(CHUNKS):
            for slot in (0, 3, 6):
                first_hop(par, chunk, slot).wait_send()
            for slot in (1, 2, 4, 5):
                next_hop(par, chunk, slot).wait_send()
            y_swap(par, chunk).wait_send()

    def copies_sent(par):
        for chunk in range(CHUNKS):
            for slot in range(7):
                spread_hop(par, chunk, slot).wait_send()

    def iteration(k, carry):
        par = lax.rem(k, 2)
        old = 1 - par
        last = k == ITERS - 1
        zeros = jnp.zeros((8, TARGETS), jnp.float32)

        def multiply(chunk, carry):
            def block_of_chunk(block, carry):
                rows = pl.ds(pl.multiple_of(chunk * CHUNK + block * BLOCK, BLOCK), BLOCK)
                product = jnp.dot(cache[rows, :], right_side[...], preferred_element_type=jnp.float32)
                copies[rows, :] = product
                rounded[rows, :] = product.astype(jnp.bfloat16)
                summed[rows, :] = product + dual[rows, :]
                return carry

            lax.fori_loop(0, CHUNK // BLOCK, block_of_chunk, 0)
            first_hops(par, chunk)
            return carry

        lax.fori_loop(0, CHUNKS, multiply, 0)
        share[...] = jnp.dot(tile[...], rounded[...], preferred_element_type=jnp.float32)
        stage_a(par)


        for chunk in range(CHUNKS):
            first_hop(par, chunk, 3).wait_recv()
            add_here(par, chunk, 3, -2)
            next_hop(par, chunk, 4).start()
            first_hop(par, chunk, 0).wait_recv()
            first_hop(par, chunk, 6).wait_recv()
            add_here(par, chunk, 0, 2)
            next_hop(par, chunk, 1).start()
            if chunk == 1:
                stage_b(par)


        @pl.when(last)
        def _():
            def from_old(block, total):
                rows = pl.ds(pl.multiple_of(block * HEIGHT, HEIGHT), HEIGHT)
                return total + in_rows((copies[rows, :] - center[old, rows, :]) ** 2)

            spread_sum[...] = lax.fori_loop(0, WIDTH // HEIGHT, from_old, zeros)
            for row in range(ITERS - 1):
                for lane in range(2):
                    note(row, lane, tally[row, lane])

        for chunk in range(CHUNKS):
            next_hop(par, chunk, 4).wait_recv()
            add_here(par, chunk, 4, -1)
            next_hop(par, chunk, 5).start()
            next_hop(par, chunk, 1).wait_recv()
            add_here(par, chunk, 1, 1)
            next_hop(par, chunk, 2).start()
            if chunk == 1:
                stage_c(par)


        @pl.when(k > 0)
        def _():
            copies_sent(old)

        for chunk in range(CHUNKS):
            next_hop(par, chunk, 5).wait_recv()
            next_hop(par, chunk, 2).wait_recv()
            y_out[par, chunk] = summed[piece(chunk, 0), :] + (chain[par, chunk, 2] + chain[par, chunk, 5])
            y_swap(par, chunk).start()
            if chunk == 1:
                stage_d(par)


        def record_step(stage):
            @pl.when(last)
            def _():
                record_finish(stage)
                record_start(stage + 1)

        motion = shift = zeros
        for chunk in range(CHUNKS):
            y_swap(par, chunk).wait_recv()
            average = (y_out[par, chunk] + y_in[par, chunk]) * (1.0 / 16)
            clipped = jnp.clip(average, -threshold, threshold)
            updated = average - clipped
            where = piece(chunk, 0)
            center[par, where, :] = updated
            spread_hop(par, chunk, 0).start()
            spread_hop(par, chunk, 3).start()
            before = center[old, where, :]
            moved = updated - before
            if chunk == 1:
                stage_e(par)
            motion = motion + in_rows(moved**2)
            ahead = average - clip_piece[chunk] - before
            shift = shift + in_rows(moved * (8.0 * moved - 16.0 * ahead))
            clip_piece[chunk] = clipped
        tally[k, 1] = 8.0 * motion
        sums_sent(par)

        for chunk in range(CHUNKS):
            for slot in (0, 3):
                spread_hop(par, chunk, slot).wait_recv()
                spread_hop(par, chunk, slot + 1).start()
        stage_f(par)
        fitted = (observed[...] + row_dual[...] + share_mean[par]) * (1.0 / 17)
        drift = share_mean[par] - fitted
        drift_sum = in_rows(drift**2)

        @pl.when(last)
        def _():
            note(ITERS - 1, 0, spread_sum[...] + (shift + drift_sum))
            note(ITERS - 1, 1, tally[ITERS - 1, 1])
            record_start(0)
            fitted_ref[...] = fitted * 16.0

        @pl.when(k < ITERS - 1)
        def _():
            fitted_mean[...] = fitted
            row_dual[...] = row_dual[...] + drift
            pull(par)

        for chunk in range(CHUNKS):
            spread_hop(par, chunk, 1).wait_recv()
            spread_hop(par, chunk, 6).start()
            spread_hop(par, chunk, 2).start()
            spread_hop(par, chunk, 4).wait_recv()
            spread_hop(par, chunk, 5).start()
            if chunk % 2 == 1:
                record_step(chunk // 2)

        for chunk in range(CHUNKS):
            spread_hop(par, chunk, 2).wait_recv()
            spread_hop(par, chunk, 5).wait_recv()
            spread_hop(par, chunk, 6).wait_recv()
            if chunk == 1:
                record_step(2)
            rows = chunk_rows(chunk)

            @pl.when(last)
            def _():
                pltpu.make_async_copy(center.at[par, rows], coef_hbm.at[rows], store_sem.at[chunk]).start()

            @pl.when(k < ITERS - 1)
            def _():
                def settle(block, part):
                    rows = pl.ds(pl.multiple_of(chunk * CHUNK + block * SMALL, SMALL), SMALL)
                    new = center[par, rows, :]
                    new_dual = summed[rows, :] - new
                    dual[rows, :] = new_dual
                    right_side[rows, :] = (new - new_dual + pulled[rows, :]).astype(jnp.bfloat16)
                    return part + in_rows((copies[rows, :] - new) ** 2)

                part = lax.fori_loop(0, CHUNK // SMALL, settle, zeros)
                spread_sum[...] = (drift_sum if chunk == 0 else spread_sum[...]) + part

        @pl.when(last)
        def _():
            record_finish(3)
            record_start(4)

        tally[k, 0] = spread_sum[...]

        return carry

    lax.fori_loop(0, ITERS, iteration, 0)
    copies_sent((ITERS - 1) % 2)
    record_finish(4)
    history_ref[...] = record[0:ITERS, 0:2] * (1.0 / NORMALIZER)
    for chunk in range(CHUNKS):
        rows = chunk_rows(chunk)
        pltpu.make_async_copy(center.at[(ITERS - 1) % 2, rows], coef_hbm.at[rows], store_sem.at[chunk]).wait()


def local(matrix, inverse, target, penalty, consensus, copy_duals, fit_parts, fit_mean, fit_duals):
    f32, bf16 = jnp.float32, jnp.bfloat16
    anywhere = pl.BlockSpec(memory_space=pltpu.HBM)
    inside = pl.BlockSpec(memory_space=pltpu.VMEM)
    dma = pltpu.SemaphoreType.DMA

    def v(*shape, dtype=f32):
        return pltpu.VMEM(shape, dtype)

    return pl.pallas_call(
        kernel,
        name="admm",
        out_shape=(
            jax.ShapeDtypeStruct((WIDTH, TARGETS), f32),
            jax.ShapeDtypeStruct((HEIGHT, TARGETS), f32),
            jax.ShapeDtypeStruct((ITERS, 2), f32),
        ),
        in_specs=[anywhere, anywhere, anywhere, inside, anywhere, anywhere, anywhere, anywhere, anywhere],
        out_specs=(anywhere, inside, inside),
        scratch_shapes=[
            v(WIDTH, WIDTH, dtype=bf16),
            v(HEIGHT, WIDTH, dtype=bf16),
            v(WIDTH, HEIGHT, dtype=bf16),
            v(2, WIDTH, TARGETS),
            v(WIDTH, TARGETS),
            v(WIDTH, TARGETS),
            v(WIDTH, TARGETS),
            v(WIDTH, TARGETS),
            v(WIDTH, TARGETS, dtype=bf16),
            v(WIDTH, TARGETS, dtype=bf16),
            v(HEIGHT, TARGETS),
            v(2, HEIGHT, TARGETS),
            v(HEIGHT, TARGETS),
            v(HEIGHT, TARGETS),
            v(HEIGHT, TARGETS),
            v(2, CHUNKS, 7, PIECE, TARGETS),
            v(2, CHUNKS, PIECE, TARGETS),
            v(2, CHUNKS, PIECE, TARGETS),
            v(2, HALF, TARGETS),
            v(2, 3, QUARTER, TARGETS),
            v(HALF, TARGETS),
            v(QUARTER, TARGETS),
            v(2, QUARTER, TARGETS),
            v(CHUNKS, PIECE, TARGETS),
            v(8, TARGETS),
            v(ITERS, 2, 8, TARGETS),
            v(8, TARGETS),
            v(18, 8, TARGETS),
            dma((LOADS,)),
            dma((CHUNKS,)),
            dma((CHUNKS,)),
            dma((2, CHUNKS, 7)),
            dma((2, CHUNKS, 7)),
            dma((2, CHUNKS, 7)),
            dma((2, CHUNKS, 7)),
            dma((2, CHUNKS)),
            dma((2, CHUNKS)),
            dma((2, 9)),
            dma((2, 9)),
            dma((18,)),
            dma((18,)),
        ],
        compiler_params=pltpu.CompilerParams(
            collective_id=0, has_side_effects=True, vmem_limit_bytes=60 * 1024 * 1024
        ),
    )(inverse, matrix, target, penalty.reshape(1, TARGETS), consensus, copy_duals, fit_parts, fit_mean, fit_duals)


def solution(mesh):
    split = Mesh(mesh.devices.reshape(SIZES), AXES)
    return jax.shard_map(
        local,
        mesh=split,
        in_specs=(
            P(ROWS, COLS),
            P(ROWS, COLS),
            P(ROWS, None),
            P(),
            P(COLS, None),
            P(ROWS, COLS, None),
            P(COLS, ROWS, None),
            P(ROWS, None),
            P(ROWS, None),
        ),
        out_specs=(P(COLS, None), P(ROWS, None), P()),
        check_vma=False,
    )
```

```python
import jax
import jax.numpy as jnp
from jax import lax
from jax.experimental import pallas as pl
from jax.experimental.pallas import tpu as pltpu
from jax.sharding import Mesh
from jax.sharding import PartitionSpec as P

ITERS = 5
ROWS = ("rows_0", "rows_1")
COLS = ("cols_0", "cols_1", "cols_2")
AXES = ("rows_0", "rows_1", "cols_0", "cols_1", "cols_2")
SIZES = (2, 8, 4, 2, 2)
MESH = pl.DeviceIdType.MESH
GROUPS = (("cols_2",), ("rows_0",), ("cols_1",), ("cols_0",), ("rows_1",))

WIDTH = 2048
HEIGHT = 256
TARGETS = 128
NZ = 8
CHUNKS = 4
CHUNK = WIDTH // CHUNKS
PIECE = CHUNK // NZ
BLOCK = 512
SMALL = 512
HALF = HEIGHT // 2
QUARTER = HALF // 4
LOADS = 7
FIRST = {0: (1, 3, 1), 3: (-1, -3, 1), 6: (1, 4, 2)}
SPREAD = {0: (1, 0, 1), 1: (1, -1, 1), 2: (1, -2, 1), 3: (-1, 0, 1), 4: (-1, 1, 1), 5: (-1, 2, 1), 6: (1, -2, 2)}
NORMALIZER = 16.0 * 32768.0 * 128.0


def kernel(
    inverse_hbm, matrix_hbm, target_hbm, penalty_ref, consensus_hbm, duals_hbm, parts_hbm, mean_hbm, fit_duals_hbm,
    coef_hbm, fitted_ref, history_ref,
    cache, tile, tile_t, center, dual, summed, copies, pulled, right_side, rounded,
    share, share_mean, fitted_mean, row_dual, observed,
    chain, y_out, y_in, core_in, x_in, half_sum, quarter_sum, yh_in, clip_piece, spread_sum, tally, record, record_in,
    load_sem, cache_sem, store_sem,
    rs_send, rs_recv, ag_send, ag_recv, y_send, y_recv, s_send, s_recv, h_send, h_recv,
):
    me = tuple(lax.axis_index(axis) for axis in AXES)
    my_y, my_z, my_x, my_yh, my_core = me

    def device(**moved):
        return tuple(moved.get(axis, index) for axis, index in zip(AXES, me))

    def z_at(offset):
        return lax.rem(my_z + offset + 2 * NZ, NZ)

    core_peer = device(cols_2=1 - my_core)
    yh_peer = device(cols_1=1 - my_yh)
    y_peer = device(rows_0=1 - my_y)

    def x_peer(step):
        return device(cols_0=lax.rem(my_x + step, 4))

    def group(stage):
        axes = GROUPS[stage]
        size, index = 1, 0
        for axis in axes:
            extent = SIZES[AXES.index(axis)]
            size, index = size * extent, index * extent + me[AXES.index(axis)]
        members = {}
        for step in range(1, size):
            rest, moved = lax.rem(index + step, size), {}
            for axis in reversed(axes):
                extent = SIZES[AXES.index(axis)]
                moved[axis] = lax.rem(rest, extent)
                rest = lax.div(rest, extent)
            members[step] = device(**moved)
        return size, index, members

    peers = [peer for stage in range(len(GROUPS)) for peer in group(stage)[2].values()]
    barrier = pltpu.get_barrier_semaphore()
    for peer in peers:
        pl.semaphore_signal(barrier, inc=1, device_id=peer, device_id_type=MESH)

    loads = [
        pltpu.make_async_copy(src, dst, load_sem.at[index])
        for index, (src, dst) in enumerate(
            (
                (parts_hbm.at[0], share),
                (matrix_hbm, tile),
                (mean_hbm, fitted_mean),
                (fit_duals_hbm, row_dual),
                (consensus_hbm, center.at[1]),
                (duals_hbm.at[0], dual),
                (target_hbm, observed),
            )
        )
    ]
    for load in loads:
        load.start()

    def cache_load(chunk):
        rows = pl.ds(chunk * CHUNK, CHUNK)
        return pltpu.make_async_copy(inverse_hbm.at[rows], cache.at[rows], cache_sem.at[chunk])

    for chunk in range(CHUNKS):
        cache_load(chunk).start()

    def remote(src, dst, send, recv, where):
        return pltpu.make_async_remote_copy(
            src_ref=src, dst_ref=dst, send_sem=send, recv_sem=recv, device_id=where, device_id_type=MESH
        )

    mine = pl.ds(my_core * HALF, HALF)
    other = pl.ds((1 - my_core) * HALF, HALF)

    def quarter(x_index):
        return pl.ds(x_index * QUARTER, QUARTER)

    def piece_of_mean(x_index):
        return pl.ds(my_core * HALF + x_index * QUARTER, QUARTER)

    def core_sum(par):
        return remote(share.at[other], core_in.at[par], s_send.at[par, 0], s_recv.at[par, 0], core_peer)

    def x_sum(par, step):
        return remote(
            half_sum.at[quarter(lax.rem(my_x + step, 4))], x_in.at[par, step - 1],
            s_send.at[par, step], s_recv.at[par, step], x_peer(step),
        )

    def yh_sum(par):
        return remote(quarter_sum, yh_in.at[par], s_send.at[par, 4], s_recv.at[par, 4], yh_peer)

    def x_copy(par, step):
        return remote(
            share_mean.at[par, piece_of_mean(my_x)], share_mean.at[par, piece_of_mean(my_x)],
            s_send.at[par, 4 + step], s_recv.at[par, 4 + step], x_peer(step),
        )

    def core_copy(par):
        return remote(
            share_mean.at[par, mine], share_mean.at[par, mine], s_send.at[par, 8], s_recv.at[par, 8], core_peer
        )

    def stage_a(par):
        core_sum(par).start()

    def stage_b(par):
        core_sum(par).wait()
        half_sum[...] = share[mine, :] + core_in[par]
        for step in range(1, 4):
            x_sum(par, step).start()

    def stage_c(par):
        for step in range(1, 4):
            x_sum(par, step).wait()
        quarter_sum[...] = half_sum[quarter(my_x), :] + (x_in[par, 0] + x_in[par, 1] + x_in[par, 2])
        yh_sum(par).start()

    def stage_d(par):
        yh_sum(par).wait()
        share_mean[par, piece_of_mean(my_x), :] = (quarter_sum[...] + yh_in[par]) * (1.0 / 16)
        for step in range(1, 4):
            x_copy(par, step).start()

    def stage_e(par):
        for step in range(1, 4):
            x_copy(par, step).wait()
        core_copy(par).start()

    def stage_f(par):
        core_copy(par).wait()

    def pull(par):
        offsets = (share[...] - share_mean[par] + fitted_mean[...] - row_dual[...]).astype(jnp.bfloat16)
        pulled[...] = jnp.dot(tile_t[...], offsets, preferred_element_type=jnp.float32)

    loads[0].wait()
    pl.semaphore_wait(barrier, len(peers))
    stage_a(1)
    stage_b(1)
    loads[1].wait()

    def transpose_block(block, carry):
        columns = pl.ds(pl.multiple_of(block * HEIGHT, HEIGHT), HEIGHT)
        tile_t[columns, :] = tile[:, columns].T
        return carry

    lax.fori_loop(0, WIDTH // HEIGHT, transpose_block, 0)
    stage_c(1)
    for load in loads[2:]:
        load.wait()
    record[...] = jnp.zeros_like(record)
    clip_piece[...] = jnp.zeros_like(clip_piece)
    stage_d(1)
    stage_e(1)
    stage_f(1)
    pull(1)

    def first_right_side(block, carry):
        rows = pl.ds(pl.multiple_of(block * HEIGHT, HEIGHT), HEIGHT)
        right_side[rows, :] = (center[1, rows, :] - dual[rows, :] + pulled[rows, :]).astype(jnp.bfloat16)
        return carry

    lax.fori_loop(0, WIDTH // HEIGHT, first_right_side, 0)
    threshold = penalty_ref[...] * (1.0 / 16)
    for chunk in range(CHUNKS):
        cache_load(chunk).wait()

    z_near = {offset: z_at(offset) for offset in range(-4, 5)}
    z_device = {offset: device(rows_1=z_near[offset]) for offset in (-2, -1, 1, 2)}

    def turn(chunk):
        return 1 - 2 * (chunk % 2)

    def piece(chunk, offset):
        return pl.ds(pl.multiple_of(chunk * CHUNK + z_near[offset] * PIECE, PIECE), PIECE)

    def first_hop(par, chunk, slot):
        sign, far, hops = FIRST[slot]
        way = turn(chunk)
        return remote(
            summed.at[piece(chunk, far * way)], chain.at[par, chunk, slot],
            rs_send.at[par, chunk, slot], rs_recv.at[par, chunk, slot], z_device[sign * hops * way],
        )

    def next_hop(par, chunk, slot):
        sign = 1 if slot < 3 else -1
        return remote(
            chain.at[par, chunk, slot - 1], chain.at[par, chunk, slot],
            rs_send.at[par, chunk, slot], rs_recv.at[par, chunk, slot], z_device[sign * turn(chunk)],
        )

    def add_here(par, chunk, slot, offset):
        total = chain[par, chunk, slot] + summed[piece(chunk, offset * turn(chunk)), :]
        chain[par, chunk, slot] = total if slot > 0 else total + chain[par, chunk, 6]

    def y_swap(par, chunk):
        return remote(y_out.at[par, chunk], y_in.at[par, chunk], y_send.at[par, chunk], y_recv.at[par, chunk], y_peer)

    def spread_hop(par, chunk, slot):
        sign, owner, hops = SPREAD[slot]
        way = turn(chunk)
        where = piece(chunk, owner * way)
        return remote(
            center.at[par, where], center.at[par, where],
            ag_send.at[par, chunk, slot], ag_recv.at[par, chunk, slot], z_device[sign * hops * way],
        )

    def in_rows(values):
        return jnp.sum(values.reshape(-1, 8, TARGETS), axis=0)

    def chunk_rows(chunk):
        return slice(chunk * CHUNK, (chunk + 1) * CHUNK)

    def note(row, lane, value):
        rows = lax.broadcasted_iota(jnp.int32, (8, TARGETS), 0)
        lanes = lax.broadcasted_iota(jnp.int32, (8, TARGETS), 1)
        record[...] = record[...] + jnp.where((rows == row) & (lanes == lane), jnp.sum(value), 0.0)

    first_slot = (0, 2, 4, 6, 10)

    def record_swaps(stage):
        slot = first_slot[stage]
        size, index, members = group(stage)
        swaps = []
        for step in range(1, size):
            arriving = lax.rem(index + size - step, size)
            swaps.append(
                tuple(
                    remote(
                        record, record_in.at[slot + at], h_send.at[slot + step], h_recv.at[slot + at], members[step]
                    )
                    for at in (index, arriving)
                )
            )
        return slot, size, index, swaps

    def record_start(stage):
        slot, size, index, swaps = record_swaps(stage)
        for going, coming in swaps:
            going.start()
        record_in[slot + index] = record[...]

    def record_finish(stage):
        slot, size, index, swaps = record_swaps(stage)
        for going, coming in swaps:
            coming.wait_recv()
        for going, coming in swaps:
            going.wait_send()
        total = record_in[slot]
        for part in range(1, size):
            total = total + record_in[slot + part]
        record[...] = total

    def first_hops(par, chunk):
        way = 1 - 2 * lax.rem(chunk, 2)
        for slot in (6, 0, 3):
            sign, far, hops = FIRST[slot]
            where = pl.ds(pl.multiple_of(chunk * CHUNK + z_at(far * way) * PIECE, PIECE), PIECE)
            remote(
                summed.at[where], chain.at[par, chunk, slot],
                rs_send.at[par, chunk, slot], rs_recv.at[par, chunk, slot], device(rows_1=z_at(sign * hops * way)),
            ).start()

    def sums_sent(par):
        for chunk in range(CHUNKS):
            for slot in (0, 3, 6):
                first_hop(par, chunk, slot).wait_send()
            for slot in (1, 2, 4, 5):
                next_hop(par, chunk, slot).wait_send()
            y_swap(par, chunk).wait_send()

    def copies_sent(par):
        for chunk in range(CHUNKS):
            for slot in range(7):
                spread_hop(par, chunk, slot).wait_send()

    def iteration(k, carry):
        par = lax.rem(k, 2)
        old = 1 - par
        last = k == ITERS - 1
        zeros = jnp.zeros((8, TARGETS), jnp.float32)

        def multiply(chunk, carry):
            def block_of_chunk(block, carry):
                rows = pl.ds(pl.multiple_of(chunk * CHUNK + block * BLOCK, BLOCK), BLOCK)
                product = jnp.dot(cache[rows, :], right_side[...], preferred_element_type=jnp.float32)
                copies[rows, :] = product
                rounded[rows, :] = product.astype(jnp.bfloat16)
                summed[rows, :] = product + dual[rows, :]
                return carry

            lax.fori_loop(0, CHUNK // BLOCK, block_of_chunk, 0)
            first_hops(par, chunk)
            return carry

        lax.fori_loop(0, CHUNKS, multiply, 0)
        share[...] = jnp.dot(tile[...], rounded[...], preferred_element_type=jnp.float32)
        stage_a(par)


        for chunk in range(CHUNKS):
            first_hop(par, chunk, 3).wait_recv()
            add_here(par, chunk, 3, -2)
            next_hop(par, chunk, 4).start()
            first_hop(par, chunk, 0).wait_recv()
            first_hop(par, chunk, 6).wait_recv()
            add_here(par, chunk, 0, 2)
            next_hop(par, chunk, 1).start()
            if chunk == 1:
                stage_b(par)


        @pl.when(last)
        def _():
            def from_old(block, total):
                rows = pl.ds(pl.multiple_of(block * HEIGHT, HEIGHT), HEIGHT)
                return total + in_rows((copies[rows, :] - center[old, rows, :]) ** 2)

            spread_sum[...] = lax.fori_loop(0, WIDTH // HEIGHT, from_old, zeros)
            for row in range(ITERS - 1):
                for lane in range(2):
                    note(row, lane, tally[row, lane])

        for chunk in range(CHUNKS):
            next_hop(par, chunk, 4).wait_recv()
            add_here(par, chunk, 4, -1)
            next_hop(par, chunk, 5).start()
            next_hop(par, chunk, 1).wait_recv()
            add_here(par, chunk, 1, 1)
            next_hop(par, chunk, 2).start()
            if chunk == 1:
                stage_c(par)


        @pl.when(k > 0)
        def _():
            copies_sent(old)

        for chunk in range(CHUNKS):
            next_hop(par, chunk, 5).wait_recv()
            next_hop(par, chunk, 2).wait_recv()
            y_out[par, chunk] = summed[piece(chunk, 0), :] + (chain[par, chunk, 2] + chain[par, chunk, 5])
            y_swap(par, chunk).start()
            if chunk == 1:
                stage_d(par)


        def record_step(stage):
            @pl.when(last)
            def _():
                record_finish(stage)
                record_start(stage + 1)

        motion = shift = zeros
        for chunk in range(CHUNKS):
            y_swap(par, chunk).wait_recv()
            average = (y_out[par, chunk] + y_in[par, chunk]) * (1.0 / 16)
            clipped = jnp.clip(average, -threshold, threshold)
            updated = average - clipped
            where = piece(chunk, 0)
            center[par, where, :] = updated
            spread_hop(par, chunk, 0).start()
            spread_hop(par, chunk, 3).start()
            before = center[old, where, :]
            moved = updated - before
            if chunk == 1:
                stage_e(par)
            motion = motion + in_rows(moved**2)
            ahead = average - clip_piece[chunk] - before
            shift = shift + in_rows(moved * (8.0 * moved - 16.0 * ahead))
            clip_piece[chunk] = clipped
        tally[k, 1] = 8.0 * motion
        sums_sent(par)

        for chunk in range(CHUNKS):
            for slot in (0, 3):
                spread_hop(par, chunk, slot).wait_recv()
                spread_hop(par, chunk, slot + 1).start()
        stage_f(par)
        fitted = (observed[...] + row_dual[...] + share_mean[par]) * (1.0 / 17)
        drift = share_mean[par] - fitted
        drift_sum = in_rows(drift**2)

        @pl.when(last)
        def _():
            note(ITERS - 1, 0, spread_sum[...] + (shift + drift_sum))
            note(ITERS - 1, 1, tally[ITERS - 1, 1])
            record_start(0)
            fitted_ref[...] = fitted * 16.0

        for chunk in range(CHUNKS):
            spread_hop(par, chunk, 1).wait_recv()
            spread_hop(par, chunk, 6).start()
            spread_hop(par, chunk, 2).start()
            spread_hop(par, chunk, 4).wait_recv()
            spread_hop(par, chunk, 5).start()
            if chunk % 2 == 1:
                record_step(chunk // 2)

        @pl.when(k < ITERS - 1)
        def _():
            fitted_mean[...] = fitted
            row_dual[...] = row_dual[...] + drift
            pull(par)

        for chunk in range(CHUNKS):
            spread_hop(par, chunk, 2).wait_recv()
            spread_hop(par, chunk, 5).wait_recv()
            spread_hop(par, chunk, 6).wait_recv()
            if chunk == 1:
                record_step(2)
            rows = chunk_rows(chunk)

            @pl.when(last)
            def _():
                pltpu.make_async_copy(center.at[par, rows], coef_hbm.at[rows], store_sem.at[chunk]).start()

            @pl.when(k < ITERS - 1)
            def _():
                def settle(block, part):
                    rows = pl.ds(pl.multiple_of(chunk * CHUNK + block * SMALL, SMALL), SMALL)
                    new = center[par, rows, :]
                    new_dual = summed[rows, :] - new
                    dual[rows, :] = new_dual
                    right_side[rows, :] = (new - new_dual + pulled[rows, :]).astype(jnp.bfloat16)
                    return part + in_rows((copies[rows, :] - new) ** 2)

                part = lax.fori_loop(0, CHUNK // SMALL, settle, zeros)
                spread_sum[...] = (drift_sum if chunk == 0 else spread_sum[...]) + part

        @pl.when(last)
        def _():
            record_finish(3)
            record_start(4)

        tally[k, 0] = spread_sum[...]

        return carry

    lax.fori_loop(0, ITERS, iteration, 0)
    copies_sent((ITERS - 1) % 2)
    record_finish(4)
    history_ref[...] = record[0:ITERS, 0:2] * (1.0 / NORMALIZER)
    for chunk in range(CHUNKS):
        rows = chunk_rows(chunk)
        pltpu.make_async_copy(center.at[(ITERS - 1) % 2, rows], coef_hbm.at[rows], store_sem.at[chunk]).wait()


def local(matrix, inverse, target, penalty, consensus, copy_duals, fit_parts, fit_mean, fit_duals):
    f32, bf16 = jnp.float32, jnp.bfloat16
    anywhere = pl.BlockSpec(memory_space=pltpu.HBM)
    inside = pl.BlockSpec(memory_space=pltpu.VMEM)
    dma = pltpu.SemaphoreType.DMA

    def v(*shape, dtype=f32):
        return pltpu.VMEM(shape, dtype)

    return pl.pallas_call(
        kernel,
        name="admm",
        out_shape=(
            jax.ShapeDtypeStruct((WIDTH, TARGETS), f32),
            jax.ShapeDtypeStruct((HEIGHT, TARGETS), f32),
            jax.ShapeDtypeStruct((ITERS, 2), f32),
        ),
        in_specs=[anywhere, anywhere, anywhere, inside, anywhere, anywhere, anywhere, anywhere, anywhere],
        out_specs=(anywhere, inside, inside),
        scratch_shapes=[
            v(WIDTH, WIDTH, dtype=bf16),
            v(HEIGHT, WIDTH, dtype=bf16),
            v(WIDTH, HEIGHT, dtype=bf16),
            v(2, WIDTH, TARGETS),
            v(WIDTH, TARGETS),
            v(WIDTH, TARGETS),
            v(WIDTH, TARGETS),
            v(WIDTH, TARGETS),
            v(WIDTH, TARGETS, dtype=bf16),
            v(WIDTH, TARGETS, dtype=bf16),
            v(HEIGHT, TARGETS),
            v(2, HEIGHT, TARGETS),
            v(HEIGHT, TARGETS),
            v(HEIGHT, TARGETS),
            v(HEIGHT, TARGETS),
            v(2, CHUNKS, 7, PIECE, TARGETS),
            v(2, CHUNKS, PIECE, TARGETS),
            v(2, CHUNKS, PIECE, TARGETS),
            v(2, HALF, TARGETS),
            v(2, 3, QUARTER, TARGETS),
            v(HALF, TARGETS),
            v(QUARTER, TARGETS),
            v(2, QUARTER, TARGETS),
            v(CHUNKS, PIECE, TARGETS),
            v(8, TARGETS),
            v(ITERS, 2, 8, TARGETS),
            v(8, TARGETS),
            v(18, 8, TARGETS),
            dma((LOADS,)),
            dma((CHUNKS,)),
            dma((CHUNKS,)),
            dma((2, CHUNKS, 7)),
            dma((2, CHUNKS, 7)),
            dma((2, CHUNKS, 7)),
            dma((2, CHUNKS, 7)),
            dma((2, CHUNKS)),
            dma((2, CHUNKS)),
            dma((2, 9)),
            dma((2, 9)),
            dma((18,)),
            dma((18,)),
        ],
        compiler_params=pltpu.CompilerParams(
            collective_id=0, has_side_effects=True, vmem_limit_bytes=60 * 1024 * 1024
        ),
    )(inverse, matrix, target, penalty.reshape(1, TARGETS), consensus, copy_duals, fit_parts, fit_mean, fit_duals)


def solution(mesh):
    split = Mesh(mesh.devices.reshape(SIZES), AXES)
    return jax.shard_map(
        local,
        mesh=split,
        in_specs=(
            P(ROWS, COLS),
            P(ROWS, COLS),
            P(ROWS, None),
            P(),
            P(COLS, None),
            P(ROWS, COLS, None),
            P(COLS, ROWS, None),
            P(ROWS, None),
            P(ROWS, None),
        ),
        out_specs=(P(COLS, None), P(ROWS, None), P()),
        check_vma=False,
    )
```
